32 devices in a mesh: rep: 16 (over z, x, core), shard: 2 (over y).
Axes of the slice: x: 2, y: 2, z: 4, core: 2. Of those that a mesh axis runs over, the one named last changes fastest.
Arguments:
- tokens: bfloat16 [32, 197, 512], P(('rep', 'shard')), may hold values from -6 to 6
- norm_one: bfloat16 [512], P('shard'), may hold values from 0.099609375 to 1.8984375
- w_qkv: bfloat16 [512, 1536], P('shard'), may hold values from -0.25 to 0.25
- w_attn: bfloat16 [512, 512], P('shard'), may hold values from -1 to 1
- norm_two: bfloat16 [512], P('shard'), may hold values from 0.099609375 to 1.8984375
- w_gate: bfloat16 [512, 4], P('shard'), may hold values from -0.1875 to 0.1875
- w_expin: bfloat16 [4, 512, 2048], P(None, 'shard'), may hold values from -0.25 to 0.25
- w_expout: bfloat16 [4, 2048, 512], P(None, 'shard'), may hold values from -0.125 to 0.125
- routes: int32 [32, 197, 2], P(('rep', 'shard')), may hold values from 0 to 3, all different within a row
- cotangent: bfloat16 [32, 197, 512], P(('rep', 'shard')), may hold values from -6 to 6
Outputs:
- output: bfloat16 [32, 197, 512], P(('rep', 'shard'))
- grad_tokens: bfloat16 [32, 197, 512], P(('rep', 'shard'))
- grad_norm_one: float32 [512], P('shard')
- grad_qkv: float32 [512, 1536], P('shard')
- grad_attn: float32 [512, 512], P('shard')
- grad_norm_two: float32 [512], P('shard')
- grad_gate: float32 [512, 4], P('shard')
- grad_expin: float32 [4, 512, 2048], P(None, 'shard')
- grad_expout: float32 [4, 2048, 512], P(None, 'shard')
The draws below stay inside these ranges and needn't reach their ends.
Inputs may be any that keep to these rules, and one draw needn't show every extreme that they name: `routes`: each token names two different experts; every expert is named by some token.
All inputs are finite; a program needn't handle non-finite values.
Results may differ from the reference program's by a relative error of at most 0.024.
Values may be sent and summed in bfloat16 or wider, within the bound.
A program may use at most 192 MiB of HBM per device.

```python
import jax
import jax.numpy as jnp
from jax import lax

D = 512
HEADS = 8
HEAD_DIM = 64
FF = 2048
EXPERTS = 4
SEQ = 197
IMAGES = 32


def level_of(rng, shape, shards, least, largest):
    level, own = 1.0, jax.random.fold_in(rng, 6)
    for position, shards_of in shards:
        heights = jnp.exp(jax.random.uniform(jax.random.fold_in(own, position), (shards_of,), jnp.float32, least / len(shards), largest / len(shards)))
        level = level * jnp.repeat(heights, shape[position] // shards_of).reshape([-1 if axis == position else 1 for axis in range(len(shape))])
    return level


def different_ones(key, rows, number_of, top, lift):
    order = jax.random.permutation(jax.random.fold_in(key, 1), number_of)
    favour = order
    for power in range(3):
        favour = favour * favour // number_of
    favour = favour * lift // number_of
    lots = jax.random.randint(jax.random.fold_in(key, 2), (rows, number_of), 0, 4096) + favour
    sure = jax.random.permutation(jax.random.fold_in(key, 3), rows)[jnp.arange(number_of) % rows]
    lots = jnp.where(jnp.arange(rows)[:, None] == sure[None, :], 1 << 14, lots)
    priority = lots * number_of + jnp.arange(number_of)
    return lax.top_k(priority.astype(jnp.int32), top)[1].astype(jnp.int32)


def centred(own_key, dims, spread, limit, split=(), dtype=jnp.bfloat16):
    level = level_of(own_key, dims, split, -0.22, 0.18) if split else 1.0
    entries = jax.random.normal(own_key, dims, jnp.float32) * spread * level
    return jnp.minimum(jnp.maximum(entries, -limit), limit).astype(dtype)


def setup_inputs(seed: int = 0) -> dict:
    key_of = jax.random.split(jax.random.key(seed), 11)
    tokens = centred(key_of[0], (IMAGES, SEQ, D), 1.0, 6.0, ((0, 32),))
    norm_one = jnp.clip(1.0 + 0.18 * jax.random.normal(key_of[1], (D,), jnp.float32), 0.099609375, 1.8984375).astype(jnp.bfloat16)
    w_qkv = centred(key_of[2], (D, 3 * D), D ** -0.5, 0.25, ((0, 2),))
    w_attn = centred(key_of[3], (D, D), (D // 16) ** -0.5, 1.0, ((0, 2),))
    norm_two = jnp.clip(1.0 + 0.18 * jax.random.normal(key_of[4], (D,), jnp.float32), 0.099609375, 1.8984375).astype(jnp.bfloat16)
    w_gate = centred(key_of[5], (D, EXPERTS), (2 * D) ** -0.5, 0.1875, ((0, 2),))
    w_expin = centred(key_of[6], (EXPERTS, D, FF), D ** -0.5, 0.25, ((1, 2),))
    w_expout = centred(key_of[7], (EXPERTS, FF, D), FF ** -0.5, 0.125, ((1, 2),))
    routes = different_ones(key_of[8], IMAGES * SEQ, EXPERTS, 2, 0).reshape((IMAGES, SEQ, 2))
    cotangent = centred(key_of[9], (IMAGES, SEQ, D), 1.0, 6.0, ((0, 32),))
    return {"tokens": tokens, "norm_one": norm_one, "w_qkv": w_qkv, "w_attn": w_attn, "norm_two": norm_two, "w_gate": w_gate, "w_expin": w_expin, "w_expout": w_expout, "routes": routes, "cotangent": cotangent}


@jax.custom_vjp
def low(v):
    return lax.optimization_barrier(v.astype(jnp.bfloat16)).astype(jnp.float32)

@jax.custom_vjp
def low_back(v):
    return v

def low_keep(v):
    return (low(v), None)

def low_pass(kept, grad):
    return (grad,)

def back_keep(v):
    return (v, None)

def back_low(kept, grad):
    return (low(grad),)
low.defvjp(low_keep, low_pass)
low_back.defvjp(back_keep, back_low)
norm_eps = 1e-06
highest = lax.Precision.HIGHEST

def round_both(value):
    return low(low_back(value))

def layer_norm(inputs, gain_vec):
    centre = inputs - lax.optimization_barrier(jnp.mean(inputs, axis=-1, keepdims=True))
    variance = lax.optimization_barrier(jnp.mean(centre * centre, axis=-1, keepdims=True))
    return centre * lax.rsqrt(variance + norm_eps) * gain_vec

def block_forward(tokens_f, norm_one, w_qkv, w_attn, norm_two, w_gate, w_expin, w_expout, routes_blk):
    images, seq_len, model_width = tokens_f.shape
    tok_rows = images * seq_len
    resid = tokens_f.reshape(tok_rows, model_width)
    hidden_one = low(layer_norm(resid, norm_one))
    proj = round_both(jnp.dot(hidden_one, w_qkv, precision=highest))
    proj = proj.reshape(images, seq_len, 3, HEADS, HEAD_DIM)
    queries = proj[:, :, 0]
    key_rows = proj[:, :, 1]
    val_rows = proj[:, :, 2]
    scores = low_back(jnp.einsum('ishd,ithd->ihst', queries, key_rows, precision=highest) * HEAD_DIM ** (-0.5))
    soft = jax.nn.softmax(scores, axis=-1)
    attn_rows = round_both(jnp.einsum('ihst,ithd->ishd', low(soft), val_rows, precision=highest))
    attn_rows = attn_rows.reshape(tok_rows, model_width)
    mixed = resid + low_back(jnp.dot(attn_rows, w_attn, precision=highest))
    hidden_two = layer_norm(mixed, norm_two)
    logits = jnp.dot(hidden_two, w_gate, precision=highest)
    choose = (routes_blk.reshape(tok_rows, 2)[:, :, None] == jnp.arange(EXPERTS)[None, None, :]).astype(jnp.float32)
    picked = lax.optimization_barrier(jnp.sum(choose * logits[:, None, :], axis=-1))
    gates = jax.nn.softmax(picked, axis=-1)
    weight_map = lax.optimization_barrier(jnp.sum(gates[:, :, None] * choose, axis=1))
    expert_inner = low_back(jnp.einsum('td,edf->etf', low(hidden_two), w_expin, precision=highest))
    hidden_act = low(jax.nn.gelu(expert_inner, approximate=False))
    outer = low_back(jnp.einsum('etf,efd->etd', hidden_act, w_expout, precision=highest))
    combined = mixed + jnp.einsum('te,etd->td', weight_map, outer, precision=highest)
    return combined.reshape(images, seq_len, model_width)

def reference(tokens, norm_one, w_qkv, w_attn, norm_two, w_gate, w_expin, w_expout, routes, cotangent):
    weights = tuple((item.astype(jnp.float32) for item in (norm_one, w_qkv, w_attn, norm_two, w_gate, w_expin, w_expout)))
    blocks = IMAGES // 16
    tok_blocks = tokens.astype(jnp.float32).reshape(blocks, 16, SEQ, D)
    route_blocks = routes.reshape(blocks, 16, SEQ, 2)
    cot_blocks = cotangent.astype(jnp.float32).reshape(blocks, 16, SEQ, D)

    def step(carry, inputs_blk):
        tok_blk, route_blk, cot_blk = inputs_blk

        def local_fn(tok_in, *weight_list):
            return block_forward(tok_in, *weight_list, route_blk)
        out_blk, pull = jax.vjp(local_fn, tok_blk, *weights)
        grads = pull(cot_blk)
        updated = tuple((prev + new for prev, new in zip(carry, grads[1:])))
        return (updated, (out_blk.astype(jnp.bfloat16), grads[0].astype(jnp.bfloat16)))
    init = tuple((jnp.zeros_like(item) for item in weights))
    sums, stacked = lax.scan(step, init, (tok_blocks, route_blocks, cot_blocks))
    output = stacked[0].reshape(IMAGES, SEQ, D)
    grad_tokens = stacked[1].reshape(IMAGES, SEQ, D)
    return (output, grad_tokens, sums[0], sums[1], sums[2], sums[3], sums[4], sums[5], sums[6])
```

```python
from functools import partial
from types import SimpleNamespace

import jax
import jax.numpy as jnp
from jax import lax
from jax.experimental import pallas as pl
from jax.experimental.pallas import tpu as pltpu
from jax.sharding import PartitionSpec as P

HEADS = 8
HEAD_DIM = 64
GROUP = 8
NORM_EPS = 1e-06
MESH = pl.DeviceIdType.MESH
f32 = jnp.float32
bf16 = jnp.bfloat16
VMEM_BYTES = 60 << 20


def nn(a, b):
    return lax.dot_general(a, b, (((1,), (0,)), ((), ())), preferred_element_type=f32)


def nt(a, b):
    return lax.dot_general(a, b, (((1,), (1,)), ((), ())), preferred_element_type=f32)


def tn(a, b):
    return lax.dot_general(a, b, (((0,), (0,)), ((), ())), preferred_element_type=f32)


def split3(v):
    a = v.astype(bf16)
    r = v - a.astype(f32)
    b = r.astype(bf16)
    c = (r - b.astype(f32)).astype(bf16)
    return a, b, c


def geometry(mesh, tokens_shape, ff):
    g = SimpleNamespace()
    g.R, g.S = mesh.shape["rep"], mesh.shape["shard"]
    g.T = GROUP // g.S
    g.L = g.R // g.T
    g.C = min(g.T, 2)
    g.X = g.T // g.C
    g.seq = tokens_shape[1]
    g.TP = -(-g.seq // 16) * 16
    g.TK = -(-g.seq // 128) * 128
    g.ff = ff
    g.U = ff // GROUP
    g.CR = min(128, g.U, 512 // g.S)
    return g


class Where:
    def __init__(self, g):
        self.g = g
        self.rep = lax.axis_index("rep")
        self.s = lax.axis_index("shard")
        self.t = lax.rem(self.rep, g.T)
        self.red = self.rep // g.T
        self.x = self.t // g.C
        self.c = lax.rem(self.t, g.C)
        self.tp = self.s * g.T + self.t

    def sj(self, j):
        return lax.rem(self.s + j, self.g.S)

    def xj(self, j):
        return lax.rem(self.x + j, self.g.X)

    def cj(self, j):
        return lax.rem(self.c + j, self.g.C)

    def block(self, js, jx, jc):
        return self.sj(js) * self.g.T + self.xj(jx) * self.g.C + self.cj(jc)

    def dev(self, js=0, jx=0, jc=0):
        return (self.red * self.g.T + self.xj(jx) * self.g.C + self.cj(jc), self.sj(js))


def greet(w, chain):
    g = w.g
    bar = pltpu.get_barrier_semaphore()
    n = 0
    for js in range(g.S):
        for jx in range(g.X):
            for jc in range(g.C):
                if js or jx or jc:
                    pl.semaphore_signal(bar, inc=1, device_id=w.dev(js, jx, jc), device_id_type=MESH)
                    n += 1
    if chain and g.L > 1:
        @pl.when(w.red > 0)
        def _():
            pl.semaphore_signal(bar, inc=1, device_id=(w.rep - g.T, w.s), device_id_type=MESH)

        @pl.when(w.red < g.L - 1)
        def _():
            pl.semaphore_signal(bar, inc=1, device_id=(w.rep + g.T, w.s), device_id_type=MESH)

        n = n + (w.red > 0).astype(jnp.int32) + (w.red < g.L - 1).astype(jnp.int32)
    pl.semaphore_wait(bar, n)


class Sends:
    def __init__(self, sem):
        self.sem, self.n, self.open = sem, 0, []

    def go(self, src, dst, recv, dev):
        cp = pltpu.make_async_remote_copy(
            src_ref=src, dst_ref=dst, send_sem=self.sem.at[self.n], recv_sem=recv,
            device_id=dev, device_id_type=MESH,
        )
        self.n += 1
        cp.start()
        self.open.append(cp)
        return cp

    def finish(self):
        for cp in self.open:
            cp.wait_send()
        self.open = []


def arrived(ref, sem):
    pltpu.make_async_copy(ref, ref, sem).wait()


def gather_group(w, sends, at, sem, halves):
    g = w.g
    first, second = halves
    own = w.block(0, 0, 0)

    def send(js, jx, half, to):
        b = w.block(js, jx, 0)
        sends.go(at(b, half), at(b, half), sem.at[b, half], w.dev(*to))

    def core(js, jx, half):
        for j in range(1, g.C):
            send(js, jx, half, (0, 0, j))

    def wait(js, jx, jc, half):
        b = w.block(js, jx, jc)
        arrived(at(b, half), sem.at[b, half])

    for j in range(1, g.X):
        send(0, 0, first, (0, j))
    for j in range(1, g.S):
        send(0, 0, second, (j,))
    for j in range(1, g.S):
        send(0, 0, first, (j,))
    for j in range(1, g.X):
        send(0, 0, second, (0, j))
    core(0, 0, first)
    core(0, 0, second)
    for i in range(1, g.X):
        wait(0, i, 0, first)
        for j in range(1, g.S):
            send(0, i, first, (j,))
        core(0, i, first)
    for i in range(1, g.S):
        wait(i, 0, 0, second)
        for j in range(1, g.X):
            send(i, 0, second, (0, j))
        core(i, 0, second)
    for js in range(1, g.S):
        for jx in range(g.X):
            wait(js, jx, 0, first)
            core(js, jx, first)
    for jx in range(1, g.X):
        for js in range(g.S):
            wait(js, jx, 0, second)
            core(js, jx, second)
    for jc in range(1, g.C):
        for js in range(g.S):
            for jx in range(g.X):
                wait(js, jx, jc, first)
                wait(js, jx, jc, second)


def layer_norm(v, gain):
    c = v - jnp.mean(v, axis=-1, keepdims=True)
    r = lax.rsqrt(jnp.mean(c * c, axis=-1, keepdims=True) + NORM_EPS)
    xhat = c * r
    return xhat * gain, xhat, r


def norm_back(dh, xhat, r, gain):
    d = dh * gain
    return r * (
        d - jnp.mean(d, axis=-1, keepdims=True) - xhat * jnp.mean(d * xhat, axis=-1, keepdims=True)
    )


def padded(ref, rows):
    v = ref[0].astype(f32)
    return jnp.concatenate([v, jnp.zeros((rows - v.shape[0], v.shape[1]), f32)], axis=0)


def rows_of_small(small):
    pick = (
        lax.broadcasted_iota(jnp.int32, (8, 128), 0) == lax.broadcasted_iota(jnp.int32, (8, 128), 1)
    ).astype(f32).astype(bf16)
    return nt(pick, small)


def turned(v):
    r, c = v.shape
    pr, pc = -(-r // 128) * 128 - r, -(-c // 128) * 128 - c
    if pc:
        v = jnp.concatenate([v, jnp.zeros((r, pc), f32)], axis=1)
    if pr:
        v = jnp.concatenate([v, jnp.zeros((pr, v.shape[1]), f32)], axis=0)
    return v.T


def gates_of(h2, small_rows, routes_t):
    wt = small_rows.astype(bf16)
    a, b, c = split3(h2)
    logits = nt(wt, a) + nt(wt, b) + nt(wt, c)
    row = lax.broadcasted_iota(jnp.int32, logits.shape, 0).astype(f32)
    pick0 = (row == routes_t[0:1]).astype(f32)
    pick1 = (row == routes_t[1:2]).astype(f32)
    p0 = jnp.sum(pick0 * logits, axis=0, keepdims=True)
    p1 = jnp.sum(pick1 * logits, axis=0, keepdims=True)
    m = jnp.maximum(p0, p1)
    e0 = jnp.exp(p0 - m)
    e1 = jnp.exp(p1 - m)
    tot = e0 + e1
    return pick0 * (e0 / tot) + pick1 * (e1 / tot)


def attention(proj, attn, probs, g):
    D = attn.shape[1]
    low = lax.broadcasted_iota(jnp.int32, (1, 128), 1) < HEAD_DIM
    keep = lax.broadcasted_iota(jnp.int32, (1, g.TK), 1) < g.seq
    zero = jnp.zeros((), bf16)
    for p in range(D // 128):
        q2 = proj[0 : g.TP, p * 128 : (p + 1) * 128] * jnp.asarray(HEAD_DIM**-0.5, bf16)
        k2 = proj[:, D + p * 128 : D + (p + 1) * 128]
        v2 = proj[:, 2 * D + p * 128 : 2 * D + (p + 1) * 128]
        out = None
        for i in range(2):
            mine = low if i == 0 else jnp.logical_not(low)
            s = nt(jnp.where(mine, q2, zero), k2)
            s = jnp.where(keep, s, -jnp.inf)
            e = jnp.exp(s - jnp.max(s, axis=-1, keepdims=True))
            pr = e * (1.0 / jnp.sum(e, axis=-1, keepdims=True))
            probs[2 * p + i] = pr
            o = nn(pr.astype(bf16), jnp.where(mine, v2, zero))
            out = o if out is None else out + o
        attn[:, p * 128 : (p + 1) * 128] = out.astype(bf16)


def front(g, experts, ins, outs, scr):
    w = Where(g)
    tok, cot, routes, small, wqkv_h, wattn_h, wexpin_h = ins
    H, DO, WM, win, wqkv, wattn, smallf, proj, attn, probs, mixed = outs
    ssem, rsem, hsem, dsem, msem, lsem = scr
    D = tok.shape[2]
    Ds = D // g.S
    greet(w, False)
    sends = Sends(ssem)

    part = Ds // g.C
    local = []

    def rows(ref, s, lo, n):
        return ref.at[pl.ds(pl.multiple_of(s * Ds + lo, 16), n)]

    mine = pl.multiple_of(w.c * part, 16)

    def weight_out(i, src, dst):
        for j in range(1, g.S):
            d = dst.at[pl.ds(pl.multiple_of(w.s * Ds + mine, 16), part)]
            sends.go(src.at[pl.ds(mine, part)], d, rsem.at[i, w.s, w.c], w.dev(js=j))

    def weight_in(i, dst):
        for j in range(1, g.S):
            o = w.sj(j)
            d = dst.at[pl.ds(pl.multiple_of(o * Ds + mine, 16), part)]
            arrived(d, rsem.at[i, o, w.c])
            for k in range(1, g.C):
                sends.go(d, d, rsem.at[i, o, w.c], w.dev(jc=k))

    def weight_core(i, dst):
        for j in range(1, g.S):
            for k in range(1, g.C):
                o = w.sj(j)
                m = pl.multiple_of(o * Ds + w.cj(k) * part, 16)
                arrived(dst.at[pl.ds(m, part)], rsem.at[i, o, w.cj(k)])

    for i, (src, dst) in enumerate(((small, smallf), (wqkv_h, wqkv), (wattn_h, wattn))):
        weight_out(i, src, dst)
        cp = pltpu.make_async_copy(src, dst.at[pl.ds(pl.multiple_of(w.s * Ds, 16), Ds)], lsem.at[i])
        cp.start()
        local.append(cp)

    def expin_cp(src, owner, e, target):
        return (
            wexpin_h.at[e, :, pl.ds(pl.multiple_of(target * g.U, 128), g.U)],
            win.at[pl.ds(pl.multiple_of(owner * Ds, 16), Ds), e * g.U : (e + 1) * g.U],
        )

    for e in range(experts):
        src, dst = expin_cp(wexpin_h, w.s, e, w.tp)
        cp = pltpu.make_async_copy(src, dst, lsem.at[3 + e])
        cp.start()
        local.append(cp)

    def at(buf, n):
        def view(b, half):
            lo, size = ((0, n), (n, g.TP - n))[half]
            return buf.at[pl.ds(pl.multiple_of(b * g.TP + lo, 16), size)]
        return view

    own = pl.ds(pl.multiple_of(w.tp * g.TP, 16), g.TP)
    DO[own] = padded(cot, g.TP).astype(bf16)

    rt = routes[0].astype(f32)
    rt = jnp.concatenate([rt, jnp.full((g.TP - g.seq, 2), -1.0, f32)], axis=0)
    routes_t = turned(rt)[0:8, 0 : g.TP]
    resid = padded(tok, g.TP)
    c = resid - jnp.mean(resid, axis=-1, keepdims=True)
    xhat = c * lax.rsqrt(jnp.mean(c * c, axis=-1, keepdims=True) + NORM_EPS)

    for i, dst in enumerate((smallf, wqkv, wattn)):
        weight_in(i, dst)
    for cp in local[:2]:
        cp.wait()
    for i, dst in enumerate((smallf, wqkv, wattn)):
        weight_core(i, dst)
    for j in range(1, g.S):
        for e in range(experts):
            target = w.sj(j) * g.T + w.t
            src, dst = expin_cp(wexpin_h, w.s, e, target)
            sends.go(src, dst, lsem.at[8 + w.s * experts + e], w.dev(js=j))
    half0 = g.TP // 32 * 16
    small_rows = rows_of_small(smallf[...])
    gain_one = small_rows[experts : experts + 1]
    h1 = (xhat * gain_one).astype(bf16)
    for k in range(3):
        proj[0 : g.TP, k * D : (k + 1) * D] = nn(h1, wqkv[:, k * D : (k + 1) * D]).astype(bf16)
    if g.TK > g.TP:
        proj[g.TP : g.TK] = jnp.zeros((g.TK - g.TP, 3 * D), bf16)
    attention(proj, attn, probs, g)
    gather_group(w, sends, at(DO, half0), dsem, (0, 1))
    local[2].wait()
    mx = resid + nn(attn[...], wattn[...])
    mixed[...] = mx
    h2, _, _ = layer_norm(mx, small_rows[experts + 1 : experts + 2])
    H[own] = h2.astype(bf16)
    WM[w.tp] = jnp.zeros((8, g.TK), f32)
    WM[w.tp, :, 0 : g.TP] = gates_of(h2, small_rows, routes_t)
    gather_group(w, sends, at(H, half0), hsem, (0, 1))

    for js in range(g.S):
        for jx in range(g.X):
            for jc in range(g.C):
                if js or jx or jc:
                    sends.go(WM.at[w.tp], WM.at[w.tp], msem.at[w.tp], w.dev(js, jx, jc))
    for js in range(g.S):
        for jx in range(g.X):
            for jc in range(g.C):
                if js or jx or jc:
                    b = w.block(js, jx, jc)
                    arrived(WM.at[b], msem.at[b])
    for cp in local[3:]:
        cp.wait()
    for j in range(1, g.S):
        for e in range(experts):
            o = w.sj(j)
            _, dst = expin_cp(wexpin_h, o, e, w.tp)
            arrived(dst, lsem.at[8 + o * experts + e])
    sends.finish()


def erf_parts(v):
    av = jnp.abs(v)
    t = 1.0 / (1.0 + av * (0.3275911 * 0.7071067811865476))
    e = jnp.exp(v * v * -0.5)
    poly = t * (0.5 * 0.254829592 + t * (0.5 * -0.284496736 + t * (0.5 * 1.421413741 + t * (0.5 * -1.453152027 + t * (0.5 * 1.061405429)))))
    q = poly * e
    return jnp.where(v > 0, 1.0 - q, q), e * 0.3989422804014327


def middle(g, experts, ins, outs, scr):
    H, DO, WM, win, wout_h = ins
    PO, PH, DW, GO, GI = outs
    wout, INN, ACT, DG, DIN, COL, sem = scr
    w = Where(g)
    n = g.TP
    U, D = g.U, H.shape[1]
    RT = 16
    cps = []
    for e in range(experts):
        cp = pltpu.make_async_copy(
            wout_h.at[e, pl.ds(pl.multiple_of(w.t * U, 16), U)], wout.at[pl.ds(e * U, U)], sem.at[e]
        )
        cp.start()
        cps.append(cp)

    def rows(b):
        return pl.ds(pl.multiple_of(b * n, 16), n)

    @pl.loop(0, GROUP)
    def _(b):
        INN[...] = nn(H[rows(b)], win[...])
        COL[...] = turned(WM[b])

        @pl.loop(0, n // RT)
        def _(i):
            r = pl.ds(pl.multiple_of(i * RT, RT), RT)
            o = pl.ds(pl.multiple_of(b * n + i * RT, RT), RT)
            for e in range(experts):
                v = INN[r, e * U : (e + 1) * U]
                cdf, pdf = erf_parts(v)
                gate = COL[r, e : e + 1]
                ACT[o, e * U : (e + 1) * U] = (v * cdf * gate).astype(bf16)
                DG[o, e * U : (e + 1) * U] = (cdf + v * pdf) * gate

    for cp in cps:
        cp.wait()
    for e in range(experts):
        v = tn(ACT[:, e * U : (e + 1) * U], DO[...])
        k = 0
        for u in range(U // g.CR):
            for c in range(D // 256):
                GO[e * (U // g.CR) * (D // 256) + k] = v[u * g.CR : (u + 1) * g.CR, c * 256 : (c + 1) * 256]
                k += 1

    @pl.loop(0, GROUP)
    def _(b):
        INN[...] = nt(DO[rows(b)], wout[...])
        COL[...] = jnp.zeros(COL.shape, f32)

        @pl.loop(0, n // RT)
        def _(i):
            r = pl.ds(pl.multiple_of(i * RT, RT), RT)
            o = pl.ds(pl.multiple_of(b * n + i * RT, RT), RT)
            lane = lax.broadcasted_iota(jnp.int32, (RT, 128), 1)
            col = jnp.zeros((RT, 128), f32)
            for e in range(experts):
                v = INN[r, e * U : (e + 1) * U]
                a = ACT[o, e * U : (e + 1) * U].astype(f32)
                col = jnp.where(lane == e, jnp.sum(a * v, axis=-1, keepdims=True), col)
                DIN[o, e * U : (e + 1) * U] = (DG[o, e * U : (e + 1) * U] * v).astype(bf16)
            COL[r] = col

        DW[b] = COL[...].T[0:8]
        PO[rows(b)] = nn(ACT[rows(b)], wout[...]).astype(bf16)
        PH[rows(b)] = nt(DIN[rows(b)], win[...]).astype(bf16)

    Ds = D // g.S
    for e in range(experts):
        v = tn(H[...], DIN[:, e * U : (e + 1) * U])
        for s in range(g.S):
            j = lax.rem(s - w.s + g.S, g.S)
            for u in range(Ds // g.CR):
                lo = s * Ds + u * g.CR
                GI[(j * experts + e) * (Ds // g.CR) + u] = v[lo : lo + g.CR]


def scatter_group(w, sends, PB, bufs, sems, n, n0):
    g = w.g
    RC, RXA, RSA, RSB, RXB = bufs
    cs, xas, sas, sbs, xbs = sems
    n1 = n - n0

    def blk(js, jx, jc, lo=0, size=n):
        return pl.ds(pl.multiple_of(w.block(js, jx, jc) * n + lo, 16), size)

    order = [(js, jx) for js in reversed(range(g.S)) for jx in reversed(range(g.X))]
    if g.C > 1:
        for js, jx in order:
            q = w.sj(js) * g.X + w.xj(jx)
            sends.go(PB.at[blk(js, jx, 1)], RC.at[q], cs.at[q], w.dev(jc=1))
        for js, jx in order:
            q = w.sj(js) * g.X + w.xj(jx)
            arrived(RC.at[q], cs.at[q])
            r = blk(js, jx, 0)
            PB[r] = (PB[r].astype(f32) + RC[q].astype(f32)).astype(bf16)
            if jx:
                d = RXA.at[jx - 1, w.sj(js)]
                sends.go(PB.at[blk(js, jx, 0, 0, n0)], d, xas.at[jx - 1, w.sj(js)], w.dev(jx=jx))
            if js:
                d = RSB.at[js - 1, w.xj(jx)]
                sends.go(PB.at[blk(js, jx, 0, n0, n1)], d, sbs.at[js - 1, w.xj(jx)], w.dev(js=js))
    else:
        for js, jx in order:
            if jx:
                d = RXA.at[jx - 1, w.sj(js)]
                sends.go(PB.at[blk(js, jx, 0, 0, n0)], d, xas.at[jx - 1, w.sj(js)], w.dev(jx=jx))
            if js:
                d = RSB.at[js - 1, w.xj(jx)]
                sends.go(PB.at[blk(js, jx, 0, n0, n1)], d, sbs.at[js - 1, w.xj(jx)], w.dev(js=js))
    for js in reversed(range(g.S)):
        r = blk(js, 0, 0, 0, n0)
        v = PB[r].astype(f32)
        for jx in range(1, g.X):
            arrived(RXA.at[jx - 1, w.sj(js)], xas.at[jx - 1, w.sj(js)])
            v = v + RXA[jx - 1, w.sj(js)].astype(f32)
        if js:
            PB[r] = v.astype(bf16)
            sends.go(PB.at[r], RSA.at[js - 1], sas.at[js - 1], w.dev(js=js))
        else:
            top = v
    for jx in reversed(range(g.X)):
        r = blk(0, jx, 0, n0, n1)
        v = PB[r].astype(f32)
        for js in range(1, g.S):
            arrived(RSB.at[js - 1, w.xj(jx)], sbs.at[js - 1, w.xj(jx)])
            v = v + RSB[js - 1, w.xj(jx)].astype(f32)
        if jx:
            PB[r] = v.astype(bf16)
            sends.go(PB.at[r], RXB.at[jx - 1], xbs.at[jx - 1], w.dev(jx=jx))
        else:
            low = v
    for js in range(1, g.S):
        arrived(RSA.at[js - 1], sas.at[js - 1])
        top = top + RSA[js - 1].astype(f32)
    for jx in range(1, g.X):
        arrived(RXB.at[jx - 1], xbs.at[jx - 1])
        low = low + RXB[jx - 1].astype(f32)
    return top, low


def scatter_scratch(g, n, n0, width):
    n1 = n - n0
    sm1, xm1 = max(1, g.S - 1), max(1, g.X - 1)
    dma = pltpu.SemaphoreType.DMA
    return (
        [
            pltpu.VMEM((g.S * g.X, n, width), bf16),
            pltpu.VMEM((xm1, g.S, n0, width), bf16),
            pltpu.VMEM((sm1, n0, width), bf16),
            pltpu.VMEM((sm1, g.X, n1, width), bf16),
            pltpu.VMEM((xm1, n1, width), bf16),
        ],
        [dma((g.S * g.X,)), dma((xm1, g.S)), dma((sm1,)), dma((sm1, g.X)), dma((xm1,))],
    )


def attention_back(proj, probs, dattn, dproj, g):
    D = dattn.shape[1]
    low = lax.broadcasted_iota(jnp.int32, (1, 128), 1) < HEAD_DIM
    zero = jnp.zeros((), bf16)
    scale = HEAD_DIM**-0.5
    for p in range(D // 128):
        q2 = proj[0 : g.TP, p * 128 : (p + 1) * 128] * jnp.asarray(scale, bf16)
        k2 = proj[:, D + p * 128 : D + (p + 1) * 128]
        v2 = proj[:, 2 * D + p * 128 : 2 * D + (p + 1) * 128]
        d2 = dattn[:, p * 128 : (p + 1) * 128]
        dq = dk = dv = None
        for i in range(2):
            mine = low if i == 0 else jnp.logical_not(low)
            pr = probs[2 * p + i]
            da = jnp.where(mine, d2, zero)
            dp = nt(da, v2)
            ds = (pr * (dp - jnp.sum(dp * pr, axis=-1, keepdims=True))).astype(bf16)
            a = nn(ds, jnp.where(mine, k2, zero))
            b = tn(ds, jnp.where(mine, q2, zero))
            c = tn(pr.astype(bf16), da)
            dq, dk, dv = (a, b, c) if i == 0 else (dq + a, dk + b, dv + c)
        dproj[:, p * 128 : (p + 1) * 128] = (dq * scale).astype(bf16)
        dproj[:, D + p * 128 : D + (p + 1) * 128] = dk[0 : g.TP].astype(bf16)
        dproj[:, 2 * D + p * 128 : 2 * D + (p + 1) * 128] = dv[0 : g.TP].astype(bf16)


class Chain:
    def __init__(self, w, n, own, bufs, sems):
        self.w, self.n, self.own = w, n, own
        self.RU, self.RD, self.SU, self.SD, self.tot = bufs
        self.ru, self.rd, self.su, self.sd = sems
        g = w.g
        self.up, self.down = w.red, g.L - 1 - w.red
        self.most = jnp.maximum(self.up, self.down)

    def _copy(self, k, upward):
        w, g = self.w, self.w.g
        src, dst, ss, rs, d = (self.SU, self.RU, self.su, self.ru, g.T) if upward else (self.SD, self.RD, self.sd, self.rd, -g.T)
        return pltpu.make_async_remote_copy(
            src_ref=src.at[k], dst_ref=dst.at[k], send_sem=ss.at[k], recv_sem=rs.at[k],
            device_id=(w.rep + d, w.s), device_id_type=MESH,
        )

    def step(self, i, lag):
        for upward in (True, False):
            behind, ahead = (self.up, self.down) if upward else (self.down, self.up)
            R, sem, S = (self.RU, self.ru, self.SU) if upward else (self.RD, self.rd, self.SD)
            k = i - lag * behind
            ok = (k >= 0) & (k < self.n)

            @pl.when(ok & (behind > 0))
            def _():
                arrived(R.at[k], sem.at[k])

            @pl.when(ok & (behind > 0) & (ahead > 0))
            def _():
                S[k] = (self.own(k) + R[k].astype(f32)).astype(bf16)

            @pl.when(ok & (behind == 0) & (ahead > 0))
            def _():
                S[k] = self.own(k).astype(bf16)

            @pl.when(ok & (ahead > 0))
            def _():
                self._copy(k, upward).start()

    def total(self, k, store):
        self.tot[...] = self.own(k)

        @pl.when(self.up > 0)
        def _():
            self.tot[...] += self.RU[k].astype(f32)

        @pl.when(self.down > 0)
        def _():
            self.tot[...] += self.RD[k].astype(f32)

        store(self.tot[...].astype(bf16))

    def finish(self):
        @pl.loop(0, self.n)
        def _(k):
            @pl.when(self.down > 0)
            def _():
                self._copy(k, True).wait_send()

            @pl.when(self.up > 0)
            def _():
                self._copy(k, False).wait_send()


def back(g, experts, ins, outs, scr):
    w = Where(g)
    (PO, PH, DW, GO, GI, mixed, proj, attn, probs, tok, cot, WM, smallf, wqkv, wattn) = ins
    out, gtok, gqkv, gattn, gsmall, gin_h, gout_h = outs
    (PHs, POs, DWr, dattn, dproj, M, dmix, FM, FO, FI, chain_b, mchain_b, rs_h, rs_o, rs_m, stage, ssem, wsem, fsem, lsem, chain_s, mchain_s, ph_s, po_s, m_s) = scr
    D = tok.shape[2]
    n = g.TP
    n0 = n // 32 * 16
    Ds = D // g.S
    U = g.U
    CR = g.CR
    L = g.L
    greet(w, True)
    sends = Sends(ssem)
    for js in range(g.S):
        for jx in range(g.X):
            for jc in range(g.C):
                if js or jx or jc:
                    sends.go(DW.at[w.block(js, jx, jc)], DWr.at[w.tp], wsem.at[w.tp], w.dev(js, jx, jc))
    cp1 = pltpu.make_async_copy(PH, PHs, lsem.at[0])
    cp1.start()
    cp2 = pltpu.make_async_copy(PO, POs, lsem.at[1])
    cp2.start()
    cp1.wait()
    dh_top, dh_low = scatter_group(w, sends, PHs, rs_h, ph_s, n, n0)
    dh2 = jnp.concatenate([dh_top, dh_low], axis=0)
    gdg = DW[w.tp]
    for js in range(g.S):
        for jx in range(g.X):
            for jc in range(g.C):
                if js or jx or jc:
                    b = w.block(js, jx, jc)
                    arrived(DWr.at[b], wsem.at[b])
                    gdg = gdg + DWr[b]
    small = smallf[...]
    small_rows = rows_of_small(small)
    gain_one = small_rows[experts : experts + 1]
    gain_two = small_rows[experts + 1 : experts + 2]
    dlt = gdg - WM[w.tp] * jnp.sum(gdg, axis=0, keepdims=True)
    dl = turned(dlt)[0:n]
    da, db, dc = split3(dl)
    dh2 = dh2 + nt(da, small) + nt(db, small) + nt(dc, small)
    h2, xhat2, r2 = layer_norm(mixed[...], gain_two)
    ha, hb, _ = split3(h2)
    ggate = tn(ha, da) + tn(hb, da) + tn(ha, db)
    gtwo = jnp.sum(dh2 * xhat2, axis=0, keepdims=True)
    dmixed = padded(cot, n) + norm_back(dh2, xhat2, r2, gain_two)
    dmix[...] = dmixed
    dlow = dmixed.astype(bf16)
    dattn[...] = nt(dlow, wattn[...]).astype(bf16)
    M[:, 3 * D : 4 * D] = tn(attn[...], dlow).astype(bf16)
    attention_back(proj, probs, dattn, dproj, g)
    h1, xhat1, r1 = layer_norm(padded(tok, n), gain_one)
    h1b = h1.astype(bf16)
    for k in range(3):
        M[:, k * D : (k + 1) * D] = tn(h1b, dproj[:, k * D : (k + 1) * D]).astype(bf16)
    dh1 = nt(dproj[...], wqkv[...])
    gone = jnp.sum(dh1 * xhat1, axis=0, keepdims=True)
    gtok[0] = (dmix[...] + norm_back(dh1, xhat1, r1, gain_one))[0 : g.seq].astype(bf16)
    rows8 = jnp.concatenate([jnp.zeros((experts, D), f32), gone, gtwo, jnp.zeros((126 - experts, D), f32)], axis=0)
    M[:, 4 * D :] = (ggate + rows8.T).astype(bf16)
    cp2.wait()
    o_top, o_low = scatter_group(w, sends, POs, rs_o, po_s, n, n0)
    out[0] = (mixed[...] + jnp.concatenate([o_top, o_low], axis=0))[0 : g.seq].astype(bf16)
    nm = D // GROUP
    m_top, m_low = scatter_group(w, sends, M, rs_m, m_s, nm, nm // 2)
    mown = mchain_b[5]
    q = nm // 4
    mown[0] = m_top[0:q]
    mown[1] = m_top[q:]
    mown[2] = m_low[0:q]
    mown[3] = m_low[q:]

    NO = GO.shape[0]
    NI = GI.shape[0]
    per_j = NI // g.S
    cu, cc = U // CR, D // 256
    ci = Ds // CR

    def own(k):
        return G_all[k]

    G_all = chain_b[5]
    cpo = pltpu.make_async_copy(GO, G_all.at[pl.ds(0, NO)], lsem.at[2])
    cpi = pltpu.make_async_copy(GI, G_all.at[pl.ds(NO, NI)], lsem.at[3])
    cpo.start()
    cpi.start()
    cpo.wait()
    cpi.wait()
    ch = Chain(w, NO + NI, own, chain_b[:5], chain_s)
    lag = 2

    def out_view(k, t):
        e, r = k // (cu * cc), lax.rem(k, cu * cc)
        return FO.at[
            e,
            pl.ds(pl.multiple_of(t * U + (r // cc) * CR, 16), CR),
            pl.ds(pl.multiple_of(lax.rem(r, cc) * 256, 256), 256),
        ]

    def in_view(k, tp):
        e, u = k // ci, lax.rem(k, ci)
        return FI.at[e, pl.ds(pl.multiple_of(u * CR, 16), CR), pl.ds(pl.multiple_of(tp * U, 128), U)]

    def put(view, sem_at, jx, jc):
        cp = pltpu.make_async_remote_copy(
            src_ref=view, dst_ref=view, send_sem=fsem.at[2, 0, 0], recv_sem=sem_at, device_id=w.dev(0, jx, jc), device_id_type=MESH
        )
        cp.start()
        cp.wait_send()

    def spread(view, sem_at):
        for jx in range(1, g.X):
            put(view, sem_at, jx, 0)
        for jc in range(1, g.C):
            put(view, sem_at, 0, jc)

    def relay(view, sem_at):
        arrived(view, sem_at)
        for jc in range(1, g.C):
            put(view, sem_at, 0, jc)

    steps = NO + NI + lag * (L - 1)

    @pl.loop(0, steps)
    def _(i):
        ch.step(i, lag)
        k = i - lag * ch.most

        @pl.when((k >= 0) & (k < NO))
        def _():
            view = out_view(k, w.t)

            def store(v):
                view[...] = v

            ch.total(k, store)
            spread(view, fsem.at[0, w.tp, k])

        @pl.when((k >= NO) & (k < NO + NI))
        def _():
            j = (k - NO) // per_j
            kk = lax.rem(k - NO, per_j)
            view = in_view(kk, w.tp)
            SI = stage

            def store(v):
                SI[lax.rem(k, 2)] = v

            ch.total(k, store)
            src = SI.at[lax.rem(k, 2)]

            @pl.when(j == 0)
            def _():
                view[...] = src[...]
                spread(view, fsem.at[1, w.tp, kk])

            @pl.when(j > 0)
            def _():
                cp = pltpu.make_async_remote_copy(
                    src_ref=src, dst_ref=view, send_sem=fsem.at[2, 0, 0], recv_sem=fsem.at[1, w.tp, kk],
                    device_id=(w.rep, lax.rem(w.s + j, g.S)), device_id_type=MESH,
                )
                cp.start()
                cp.wait_send()

    for j in range(1, g.S):
        b = w.block(j, 0, 0)

        @pl.loop(0, per_j)
        def _(k):
            view = in_view(k, b)
            arrived(view, fsem.at[1, b, k])
            spread(view, fsem.at[1, b, k])

    for jx in range(1, g.X):
        b = w.block(0, jx, 0)
        t = w.xj(jx) * g.C + w.c

        @pl.loop(0, NO)
        def _(k):
            relay(out_view(k, t), fsem.at[0, b, k])

        for j in range(g.S):
            b = w.block(j, jx, 0)

            @pl.loop(0, per_j)
            def _(k):
                relay(in_view(k, b), fsem.at[1, b, k])

    for jc in range(1, g.C):
        for jx in range(g.X):
            t = w.xj(jx) * g.C + w.cj(jc)
            b = w.block(0, jx, jc)

            @pl.loop(0, NO)
            def _(k):
                arrived(out_view(k, t), fsem.at[0, b, k])

            for j in range(g.S):
                b = w.block(j, jx, jc)

                @pl.loop(0, per_j)
                def _(k):
                    arrived(in_view(k, b), fsem.at[1, b, k])

    mch = Chain(w, 4, lambda k: mown[k], mchain_b[:5], mchain_s)

    def m_view(t, k):
        return FM.at[pl.ds(pl.multiple_of(t * nm + k * q, 16), q)]

    @pl.loop(0, 4 + L - 1)
    def _(i):
        mch.step(i, 1)
        k = i - mch.most

        @pl.when((k >= 0) & (k < 4))
        def _():
            view = m_view(w.t, k)

            def store(v):
                view[...] = v

            mch.total(k, store)
            spread(view, fsem.at[3, w.t, k])

    for jx in range(1, g.X):
        t = w.xj(jx) * g.C + w.c

        @pl.loop(0, 4)
        def _(k):
            relay(m_view(t, k), fsem.at[3, t, k])

    for jc in range(1, g.C):
        for jx in range(g.X):
            t = w.xj(jx) * g.C + w.cj(jc)

            @pl.loop(0, 4)
            def _(k):
                arrived(m_view(t, k), fsem.at[3, t, k])

    gqkv[...] = FM[:, 0 : 3 * D].astype(f32)
    gattn[...] = FM[:, 3 * D : 4 * D].astype(f32)
    gsmall[...] = FM[:, 4 * D :].astype(f32)
    for e in range(experts):
        gout_h[e] = FO[e].astype(f32)
        gin_h[e] = FI[e].astype(f32)
    ch.finish()
    mch.finish()
    sends.finish()


def on_device(mesh, tokens, norm_one, w_qkv, w_attn, norm_two, w_gate, w_expin, w_expout, routes, cotangent):
    g = geometry(mesh, tokens.shape, w_expout.shape[1] * mesh.shape["shard"])
    experts = w_expin.shape[0]
    D = tokens.shape[2]
    Ds = D // g.S
    U = g.U
    n = g.TP
    N = GROUP * n
    EU = experts * U
    dma = pltpu.SemaphoreType.DMA
    vm = pl.BlockSpec(memory_space=pltpu.VMEM)
    hb = pl.BlockSpec(memory_space=pl.ANY)
    sds = jax.ShapeDtypeStruct
    small = jnp.concatenate(
        [w_gate, norm_one[:, None], norm_two[:, None], jnp.zeros((Ds, 126 - experts), bf16)], axis=1
    )
    front_out = [
        sds((N, D), bf16), sds((N, D), bf16), sds((GROUP, 8, g.TK), f32), sds((D, EU), bf16), sds((D, 3 * D), bf16),
        sds((D, D), bf16), sds((D, 128), bf16), sds((g.TK, 3 * D), bf16), sds((n, D), bf16),
        sds((HEADS, n, g.TK), f32), sds((n, D), f32),
    ]

    def body1(*refs):
        front(g, experts, refs[:7], refs[7:18], refs[18:])

    H, DO, WM, win, wqkv, wattn, smallf, proj, attn, probs, mixed = pl.pallas_call(
        body1,
        name="front",
        out_shape=front_out,
        in_specs=[vm, vm, vm, vm, hb, hb, hb],
        out_specs=[vm] * len(front_out),
        scratch_shapes=[dma((96,)), dma((3, g.S, g.C)), dma((GROUP, 2)), dma((GROUP, 2)), dma((GROUP,)), dma((8 + g.S * experts,))],
        compiler_params=pltpu.CompilerParams(collective_id=0, has_side_effects=True, vmem_limit_bytes=VMEM_BYTES),
    )(tokens, cotangent, routes, small, w_qkv, w_attn, w_expin)

    NO = experts * (U // g.CR) * (D // 256)
    NI = g.S * experts * (Ds // g.CR)
    mid_out = [sds((N, D), bf16), sds((N, D), bf16), sds((GROUP, 8, g.TK), f32), sds((NO, g.CR, 256), f32), sds((NI, g.CR, U), f32)]

    def body2(*refs):
        middle(g, experts, refs[:5], refs[5:10], refs[10:])

    PO, PH, DW, GO, GI = pl.pallas_call(
        body2,
        name="middle",
        out_shape=mid_out,
        in_specs=[vm, vm, vm, vm, hb],
        out_specs=[vm] * len(mid_out),
        scratch_shapes=[
            pltpu.VMEM((EU, D), bf16), pltpu.VMEM((n, EU), f32), pltpu.VMEM((N, EU), bf16), pltpu.VMEM((N, EU), f32),
            pltpu.VMEM((N, EU), bf16), pltpu.VMEM((g.TK, 128), f32), dma((experts,)),
        ],
        compiler_params=pltpu.CompilerParams(vmem_limit_bytes=VMEM_BYTES),
    )(H, DO, WM, win, w_expout)

    nm = D // GROUP
    MW = 4 * D + 128
    rs_h, ph_s = scatter_scratch(g, n, n // 32 * 16, D)
    rs_o, po_s = scatter_scratch(g, n, n // 32 * 16, D)
    rs_m, m_s = scatter_scratch(g, nm, nm // 2, MW)
    NC = NO + NI
    chain_b = [pltpu.VMEM((NC, g.CR, 256), bf16)] * 4 + [pltpu.VMEM((g.CR, 256), f32), pltpu.VMEM((NC, g.CR, 256), f32)]
    mchain_b = [pltpu.VMEM((4, nm // 4, MW), bf16)] * 4 + [pltpu.VMEM((nm // 4, MW), f32), pltpu.VMEM((4, nm // 4, MW), f32)]
    flat = [
        pltpu.VMEM((N, D), bf16), pltpu.VMEM((N, D), bf16), pltpu.VMEM((GROUP, 8, g.TK), f32), pltpu.VMEM((n, D), bf16),
        pltpu.VMEM((n, 3 * D), bf16), pltpu.VMEM((D, MW), bf16), pltpu.VMEM((n, D), f32), pltpu.VMEM((Ds, MW), bf16),
        pltpu.VMEM((experts, U * g.T, D), bf16), pltpu.VMEM((experts, Ds, U * GROUP), bf16),
        chain_b, mchain_b, rs_h, rs_o, rs_m,
        pltpu.VMEM((2, g.CR, 256), bf16), dma((96,)), dma((GROUP,)), dma((4, GROUP, max(NO, NI))), dma((4,)),
        [dma((NC,))] * 4, [dma((4,))] * 4, ph_s, po_s, m_s,
    ]
    leaves, tree = jax.tree.flatten(flat, is_leaf=lambda v: not isinstance(v, list))
    back_out = [
        sds(tokens.shape, bf16), sds(tokens.shape, bf16), sds((Ds, 3 * D), f32), sds((Ds, D), f32), sds((Ds, 128), f32),
        sds(w_expin.shape, f32), sds(w_expout.shape, f32),
    ]

    def body3(*refs):
        back(g, experts, refs[:15], refs[15:22], jax.tree.unflatten(tree, refs[22:]))

    out, gtok, gqkv, gattn, gsmall, gin, gout = pl.pallas_call(
        body3,
        name="back",
        out_shape=back_out,
        in_specs=[hb, hb, vm, hb, hb] + [vm] * 10,
        out_specs=[vm] * 5 + [vm, vm],
        scratch_shapes=leaves,
        compiler_params=pltpu.CompilerParams(collective_id=1, has_side_effects=True, vmem_limit_bytes=VMEM_BYTES),
    )(PO, PH, DW, GO, GI, mixed, proj, attn, probs, tokens, cotangent, WM, smallf, wqkv, wattn)
    return (
        out, gtok, gsmall[:, experts], gqkv, gattn, gsmall[:, experts + 1], gsmall[:, :experts], gin, gout,
    )


def solution(mesh):
    placed = (
        P(("rep", "shard"), None, None), P("shard"), P("shard", None), P("shard", None), P("shard"), P("shard", None),
        P(None, "shard", None), P(None, "shard", None), P(("rep", "shard"), None, None), P(("rep", "shard"), None, None),
    )
    return jax.shard_map(
        partial(on_device, mesh),
        mesh=mesh,
        in_specs=placed,
        out_specs=(
            P(("rep", "shard"), None, None), P(("rep", "shard"), None, None), P("shard"), P("shard", None),
            P("shard", None), P("shard"), P("shard", None), P(None, "shard", None), P(None, "shard", None),
        ),
        check_vma=False,
    )
```

```python
from functools import partial
from types import SimpleNamespace

import jax
import jax.numpy as jnp
from jax import lax
from jax.experimental import pallas as pl
from jax.experimental.pallas import tpu as pltpu
from jax.sharding import PartitionSpec as P

HEADS = 8
HEAD_DIM = 64
GROUP = 8
NORM_EPS = 1e-06
MESH = pl.DeviceIdType.MESH
f32 = jnp.float32
bf16 = jnp.bfloat16
VMEM_BYTES = 60 << 20


def nn(a, b):
    return lax.dot_general(a, b, (((1,), (0,)), ((), ())), preferred_element_type=f32)


def nt(a, b):
    return lax.dot_general(a, b, (((1,), (1,)), ((), ())), preferred_element_type=f32)


def tn(a, b):
    return lax.dot_general(a, b, (((0,), (0,)), ((), ())), preferred_element_type=f32)


def split3(v):
    a = v.astype(bf16)
    r = v - a.astype(f32)
    b = r.astype(bf16)
    c = (r - b.astype(f32)).astype(bf16)
    return a, b, c


def geometry(mesh, tokens_shape, ff):
    g = SimpleNamespace()
    g.R, g.S = mesh.shape["rep"], mesh.shape["shard"]
    g.T = GROUP // g.S
    g.L = g.R // g.T
    g.C = min(g.T, 2)
    g.X = g.T // g.C
    g.seq = tokens_shape[1]
    g.TP = -(-g.seq // 16) * 16
    g.TK = -(-g.seq // 128) * 128
    g.ff = ff
    g.U = ff // GROUP
    g.CR = min(128, g.U, 512 // g.S)
    return g


class Where:
    def __init__(self, g):
        self.g = g
        self.rep = lax.axis_index("rep")
        self.s = lax.axis_index("shard")
        self.t = lax.rem(self.rep, g.T)
        self.red = self.rep // g.T
        self.x = self.t // g.C
        self.c = lax.rem(self.t, g.C)
        self.tp = self.s * g.T + self.t

    def sj(self, j):
        return lax.rem(self.s + j, self.g.S)

    def xj(self, j):
        return lax.rem(self.x + j, self.g.X)

    def cj(self, j):
        return lax.rem(self.c + j, self.g.C)

    def block(self, js, jx, jc):
        return self.sj(js) * self.g.T + self.xj(jx) * self.g.C + self.cj(jc)

    def dev(self, js=0, jx=0, jc=0):
        return (self.red * self.g.T + self.xj(jx) * self.g.C + self.cj(jc), self.sj(js))


def greet(w):
    g = w.g
    bar = pltpu.get_barrier_semaphore()
    n = 0
    for js in range(g.S):
        for jx in range(g.X):
            for jc in range(g.C):
                if js or jx or jc:
                    pl.semaphore_signal(bar, inc=1, device_id=w.dev(js, jx, jc), device_id_type=MESH)
                    n += 1
    if g.L > 1:
        @pl.when(w.red > 0)
        def _():
            pl.semaphore_signal(bar, inc=1, device_id=(w.rep - g.T, w.s), device_id_type=MESH)

        @pl.when(w.red < g.L - 1)
        def _():
            pl.semaphore_signal(bar, inc=1, device_id=(w.rep + g.T, w.s), device_id_type=MESH)

        n = n + (w.red > 0).astype(jnp.int32) + (w.red < g.L - 1).astype(jnp.int32)
    pl.semaphore_wait(bar, n)


class Sends:
    def __init__(self, sem):
        self.sem, self.n, self.open = sem, 0, []

    def go(self, src, dst, recv, dev):
        cp = pltpu.make_async_remote_copy(
            src_ref=src, dst_ref=dst, send_sem=self.sem.at[self.n], recv_sem=recv,
            device_id=dev, device_id_type=MESH,
        )
        self.n += 1
        cp.start()
        self.open.append(cp)
        return cp

    def finish(self):
        for cp in self.open:
            cp.wait_send()
        self.open = []


def arrived(ref, sem):
    pltpu.make_async_copy(ref, ref, sem).wait()


def layer_norm(v, gain):
    c = v - jnp.mean(v, axis=-1, keepdims=True)
    r = lax.rsqrt(jnp.mean(c * c, axis=-1, keepdims=True) + NORM_EPS)
    xhat = c * r
    return xhat * gain, xhat, r


def norm_back(dh, xhat, r, gain):
    d = dh * gain
    return r * (
        d - jnp.mean(d, axis=-1, keepdims=True) - xhat * jnp.mean(d * xhat, axis=-1, keepdims=True)
    )


def padded(ref, rows):
    v = ref[0].astype(f32)
    return jnp.concatenate([v, jnp.zeros((rows - v.shape[0], v.shape[1]), f32)], axis=0)


def turned(v):
    r, c = v.shape
    pr, pc = -(-r // 128) * 128 - r, -(-c // 128) * 128 - c
    if pc:
        v = jnp.concatenate([v, jnp.zeros((r, pc), f32)], axis=1)
    if pr:
        v = jnp.concatenate([v, jnp.zeros((pr, v.shape[1]), f32)], axis=0)
    return v.T


def gates_of(h2, small_rows, routes_t):
    wt = small_rows.astype(bf16)
    a, b, c = split3(h2)
    logits = nt(wt, a) + nt(wt, b) + nt(wt, c)
    row = lax.broadcasted_iota(jnp.int32, logits.shape, 0).astype(f32)
    pick0 = (row == routes_t[0:1]).astype(f32)
    pick1 = (row == routes_t[1:2]).astype(f32)
    p0 = jnp.sum(pick0 * logits, axis=0, keepdims=True)
    p1 = jnp.sum(pick1 * logits, axis=0, keepdims=True)
    m = jnp.maximum(p0, p1)
    e0 = jnp.exp(p0 - m)
    e1 = jnp.exp(p1 - m)
    tot = e0 + e1
    return pick0 * (e0 / tot) + pick1 * (e1 / tot)


def attention(proj, attn, probs, g):
    D = attn.shape[1]
    low = lax.broadcasted_iota(jnp.int32, (1, 128), 1) < HEAD_DIM
    keep = lax.broadcasted_iota(jnp.int32, (1, g.TK), 1) < g.seq
    zero = jnp.zeros((), bf16)
    for p in range(D // 128):
        q2 = proj[0 : g.TP, p * 128 : (p + 1) * 128] * jnp.asarray(HEAD_DIM**-0.5, bf16)
        k2 = proj[:, D + p * 128 : D + (p + 1) * 128]
        v2 = proj[:, 2 * D + p * 128 : 2 * D + (p + 1) * 128]
        out = None
        for i in range(2):
            mine = low if i == 0 else jnp.logical_not(low)
            s = nt(jnp.where(mine, q2, zero), k2)
            s = jnp.where(keep, s, -jnp.inf)
            e = jnp.exp(s - jnp.max(s, axis=-1, keepdims=True))
            pr = e * (1.0 / jnp.sum(e, axis=-1, keepdims=True))
            probs[2 * p + i] = pr
            o = nn(pr.astype(bf16), jnp.where(mine, v2, zero))
            out = o if out is None else out + o
        attn[:, p * 128 : (p + 1) * 128] = out.astype(bf16)


def erf_parts(v):
    av = jnp.abs(v)
    t = 1.0 / (1.0 + av * (0.3275911 * 0.7071067811865476))
    e = jnp.exp(v * v * -0.5)
    poly = t * (0.5 * 0.254829592 + t * (0.5 * -0.284496736 + t * (0.5 * 1.421413741 + t * (0.5 * -1.453152027 + t * (0.5 * 1.061405429)))))
    q = poly * e
    return jnp.where(v > 0, 1.0 - q, q), e * 0.3989422804014327


def attention_back(proj, probs, dattn, dproj, g, serve):
    D = dattn.shape[1]
    low = lax.broadcasted_iota(jnp.int32, (1, 128), 1) < HEAD_DIM
    zero = jnp.zeros((), bf16)
    scale = HEAD_DIM**-0.5
    for p in range(D // 128):
        q2 = proj[0 : g.TP, p * 128 : (p + 1) * 128] * jnp.asarray(scale, bf16)
        k2 = proj[:, D + p * 128 : D + (p + 1) * 128]
        v2 = proj[:, 2 * D + p * 128 : 2 * D + (p + 1) * 128]
        d2 = dattn[:, p * 128 : (p + 1) * 128]
        dq = dk = dv = None
        for i in range(2):
            mine = low if i == 0 else jnp.logical_not(low)
            pr = probs[2 * p + i]
            da = jnp.where(mine, d2, zero)
            dp = nt(da, v2)
            ds = (pr * (dp - jnp.sum(dp * pr, axis=-1, keepdims=True))).astype(bf16)
            a = nn(ds, jnp.where(mine, k2, zero))
            b = tn(ds, jnp.where(mine, q2, zero))
            c = tn(pr.astype(bf16), da)
            dq, dk, dv = (a, b, c) if i == 0 else (dq + a, dk + b, dv + c)
        dproj[:, p * 128 : (p + 1) * 128] = (dq * scale).astype(bf16)
        dproj[:, D + p * 128 : D + (p + 1) * 128] = dk[0 : g.TP].astype(bf16)
        dproj[:, 2 * D + p * 128 : 2 * D + (p + 1) * 128] = dv[0 : g.TP].astype(bf16)
        if p % 2:
            serve(1)


class Chain:
    def __init__(self, w, n, own, bufs, sems):
        self.w, self.n, self.own = w, n, own
        self.RU, self.RD, self.SU, self.SD, self.tot = bufs
        self.ru, self.rd, self.su, self.sd = sems
        g = w.g
        self.up, self.down = w.red, g.L - 1 - w.red
        self.most = jnp.maximum(self.up, self.down)

    def _copy(self, k, upward):
        w, g = self.w, self.w.g
        src, dst, ss, rs, d = (self.SU, self.RU, self.su, self.ru, g.T) if upward else (self.SD, self.RD, self.sd, self.rd, -g.T)
        return pltpu.make_async_remote_copy(
            src_ref=src.at[k], dst_ref=dst.at[k], send_sem=ss.at[k], recv_sem=rs.at[k],
            device_id=(w.rep + d, w.s), device_id_type=MESH,
        )

    def step(self, i, lag):
        for upward in (True, False):
            behind, ahead = (self.up, self.down) if upward else (self.down, self.up)
            R, sem, S = (self.RU, self.ru, self.SU) if upward else (self.RD, self.rd, self.SD)
            k = i - lag * behind
            ok = (k >= 0) & (k < self.n)

            @pl.when(ok & (behind > 0))
            def _():
                arrived(R.at[k], sem.at[k])

            @pl.when(ok & (behind > 0) & (ahead > 0))
            def _():
                S[k] = (self.own(k) + R[k].astype(f32)).astype(bf16)

            @pl.when(ok & (behind == 0) & (ahead > 0))
            def _():
                S[k] = self.own(k).astype(bf16)

            @pl.when(ok & (ahead > 0))
            def _():
                self._copy(k, upward).start()

    def sum(self, k):
        self.tot[...] = self.own(k)

        @pl.when(self.up > 0)
        def _():
            self.tot[...] += self.RU[k].astype(f32)

        @pl.when(self.down > 0)
        def _():
            self.tot[...] += self.RD[k].astype(f32)

    def finish(self):
        @pl.loop(0, self.n)
        def _(k):
            @pl.when(self.down > 0)
            def _():
                self._copy(k, True).wait_send()

            @pl.when(self.up > 0)
            def _():
                self._copy(k, False).wait_send()


class Scatter:
    def __init__(self, w, sends, PB, n, bufs, sems):
        self.w, self.sends, self.PB, self.n = w, sends, PB, n
        self.RC, self.RS, self.RX = bufs
        self.cs, self.ss, self.xs = sems

    @staticmethod
    def scratch(g, n, width):
        sm1, xm1 = max(1, g.S - 1), max(1, g.X - 1)
        dma = pltpu.SemaphoreType.DMA
        return (
            [pltpu.VMEM((g.S * g.X, n, width), bf16), pltpu.VMEM((sm1, g.X, n, width), bf16), pltpu.VMEM((xm1, n, width), bf16)],
            [dma((g.S * g.X,)), dma((sm1, g.X)), dma((xm1,))],
        )

    def rows(self, js, jx, jc):
        return pl.ds(pl.multiple_of(self.w.block(js, jx, jc) * self.n, 16), self.n)

    def _q(self, js, jx):
        return self.w.sj(js) * self.w.g.X + self.w.xj(jx)

    def core_send(self, js, jx):
        q = self._q(js, jx)
        self.sends.go(self.PB.at[self.rows(js, jx, 1)], self.RC.at[q], self.cs.at[q], self.w.dev(jc=1))

    def core_add(self, js, jx):
        if self.w.g.C > 1:
            q = self._q(js, jx)
            arrived(self.RC.at[q], self.cs.at[q])
            r = self.rows(js, jx, 0)
            self.PB[r] = (self.PB[r].astype(f32) + self.RC[q].astype(f32)).astype(bf16)

    def s_send(self, js, jx):
        d = self.RS.at[js - 1, self.w.xj(jx)]
        self.sends.go(self.PB.at[self.rows(js, jx, 0)], d, self.ss.at[js - 1, self.w.xj(jx)], self.w.dev(js=js))

    def _s_sum(self, jx):
        v = self.PB[self.rows(0, jx, 0)].astype(f32)
        for js in range(1, self.w.g.S):
            arrived(self.RS.at[js - 1, self.w.xj(jx)], self.ss.at[js - 1, self.w.xj(jx)])
            v = v + self.RS[js - 1, self.w.xj(jx)].astype(f32)
        return v

    def x_send(self, jx):
        r = self.rows(0, jx, 0)
        self.PB[r] = self._s_sum(jx).astype(bf16)
        self.sends.go(self.PB.at[r], self.RX.at[jx - 1], self.xs.at[jx - 1], self.w.dev(jx=jx))

    def result(self):
        v = self._s_sum(0)
        for jx in range(1, self.w.g.X):
            arrived(self.RX.at[jx - 1], self.xs.at[jx - 1])
            v = v + self.RX[jx - 1].astype(f32)
        return v


class Tail:
    def __init__(self, g, w, experts, D, r):
        self.g, self.w, self.r, self.experts = g, w, r, experts
        self.U, self.CR, self.Ds = g.U, g.CR, D // g.S
        self.cu, self.cc, self.ci = g.U // g.CR, D // 256, self.Ds // g.CR
        self.NO, self.NI, self.NM = g.NO, g.NI, g.NM
        self.n = g.NO + g.NI + g.NM + 1
        self.ch = Chain(w, self.n, lambda k: r.G[k], (r.RU, r.RD, r.SU, r.SD, r.tot), r.chain_s)
        self.i = 0
        self.ready = 0
        self.d = 2
        self.total = self.n + g.LAG * (g.L - 1) + 2 * self.d

    def out_view(self, k, t):
        e, q = k // (self.cu * self.cc), lax.rem(k, self.cu * self.cc)
        return self.r.FO.at[
            e,
            pl.ds(pl.multiple_of(t * self.U + (q // self.cc) * self.CR, 16), self.CR),
            pl.ds(pl.multiple_of(lax.rem(q, self.cc) * 256, 256), 256),
        ]

    def in_view(self, k, tp):
        e, u = k // self.ci, lax.rem(k, self.ci)
        return self.r.FI.at[
            e, pl.ds(pl.multiple_of(u * self.CR, 16), self.CR), pl.ds(pl.multiple_of(tp * self.U, 128), self.U)
        ]

    def send(self, view, recv, kind, k, dev):
        pltpu.make_async_remote_copy(
            src_ref=view, dst_ref=view, send_sem=self.r.fsend.at[kind, k], recv_sem=recv, device_id=dev, device_id_type=MESH
        ).start()

    def spread(self, view, recv, kind, k):
        w, g = self.w, self.g
        if g.X > 1:
            self.send(view, recv, kind, k, w.dev(jx=1))
        if g.C > 1:
            self.send(view, recv, kind + 1, k, w.dev(jc=1))

    def relay(self, view, recv, kind, k):
        arrived(view, recv)
        if self.g.C > 1:
            self.send(view, recv, kind, k, self.w.dev(jc=1))

    def serve(self, times=1):
        for _ in range(times):
            if self.i < self.ready:
                self.step(self.i)
                self.i += 1

    def step(self, i):
        g, w, r = self.g, self.w, self.r
        NO, NI, NM = self.NO, self.NI, self.NM
        self.ch.step(i, g.LAG)
        k = i - g.LAG * self.ch.most
        tx = w.xj(1) * g.C + w.c

        def kinds(k, f_out, f_in, f_m):
            @pl.when((k >= 0) & (k < NO))
            def _():
                f_out(k)

            @pl.when((k >= NO) & (k < NO + NI))
            def _():
                f_in(k, (k - NO) // g.S, lax.rem(k - NO, g.S))

            @pl.when((k >= NO + NI) & (k < NO + NI + NM))
            def _():
                f_m(k, k - NO - NI)

        @pl.when((k >= 0) & (k < self.n))
        def _():
            self.ch.sum(k)

        def own_out(k):
            view = self.out_view(k, w.t)
            view[...] = r.tot[...].astype(bf16)
            self.spread(view, r.fo.at[w.t, k], 0, k)

        def own_in(k, kk, j):
            @pl.when(j == 0)
            def _():
                view = self.in_view(kk, w.tp)
                view[...] = r.tot[...].astype(bf16)
                self.spread(view, r.fi.at[w.tp, kk], 0, k)

            if g.S > 1:
                @pl.when(j > 0)
                def _():
                    r.RU[k] = r.tot[...].astype(bf16)
                    pltpu.make_async_remote_copy(
                        src_ref=r.RU.at[k], dst_ref=self.in_view(kk, w.tp), send_sem=r.fsend.at[0, k],
                        recv_sem=r.fi.at[w.tp, kk], device_id=(w.rep, lax.rem(w.s + j, g.S)), device_id_type=MESH,
                    ).start()

        def own_m(k, m):
            view = r.FM.at[w.t, m]
            view[...] = r.tot[...].astype(bf16)
            self.spread(view, r.fm.at[w.t, m], 0, k)

        kinds(k, own_out, own_in, own_m)

        @pl.when(k == self.n - 1)
        def _():
            r.SGo[...] = r.tot[0:8, 0 : self.Ds]

        def from_s(j):
            return lax.rem(w.s - j + g.S, g.S)

        def nothing(*_):
            pass

        if g.S > 1:
            def peer_in(k, kk, j):
                @pl.when(j > 0)
                def _():
                    b = from_s(j) * g.T + w.t
                    view = self.in_view(kk, b)
                    arrived(view, r.fi.at[b, kk])
                    self.spread(view, r.fi.at[b, kk], 2, k)

            kinds(k - self.d, nothing, peer_in, nothing)

        if g.X > 1:
            def x_out(k):
                self.relay(self.out_view(k, tx), r.fo.at[tx, k], 4, k)

            def x_in(k, kk, j):
                @pl.when(j == 0)
                def _():
                    b = w.s * g.T + tx
                    self.relay(self.in_view(kk, b), r.fi.at[b, kk], 4, k)

            def x_m(k, m):
                self.relay(r.FM.at[tx, m], r.fm.at[tx, m], 4, k)

            kinds(k - self.d, x_out, x_in, x_m)

            if g.S > 1:
                def x_peer_in(k, kk, j):
                    @pl.when(j > 0)
                    def _():
                        b = from_s(j) * g.T + tx
                        self.relay(self.in_view(kk, b), r.fi.at[b, kk], 4, k)

                kinds(k - 2 * self.d, nothing, x_peer_in, nothing)

    def finish(self):
        g, w, r = self.g, self.w, self.r
        if g.C > 1:
            for jx in range(g.X):
                t = w.xj(jx) * g.C + w.cj(1)

                @pl.loop(0, self.NO)
                def _(k):
                    arrived(self.out_view(k, t), r.fo.at[t, k])

                for js in range(g.S):
                    b = w.sj(js) * g.T + t

                    @pl.loop(0, self.NI // g.S)
                    def _(k):
                        arrived(self.in_view(k, b), r.fi.at[b, k])

                @pl.loop(0, self.NM)
                def _(m):
                    arrived(r.FM.at[t, m], r.fm.at[t, m])
        self.ch.finish()
        one = r.RU.at[0]

        @pl.loop(0, self.n - 1)
        def _(k):
            inner = (k >= self.NO) & (k < self.NO + self.NI)
            j = lax.rem(jnp.maximum(k - self.NO, 0), g.S)
            plain = jnp.logical_not(inner & (j > 0))

            def gone(kind):
                arrived(one, r.fsend.at[kind, k])

            if g.S > 1:
                @pl.when(inner & (j > 0))
                def _():
                    gone(0)
                    if g.X > 1:
                        gone(2)
                    if g.C > 1:
                        gone(3)

            @pl.when(plain)
            def _():
                if g.X > 1:
                    gone(0)
                if g.C > 1:
                    gone(1)

            if g.X > 1 and g.C > 1:
                gone(4)


def whole_step(g, experts, r):
    w = Where(g)
    D, n, U = r.tok.shape[2], g.TP, g.U
    Ds = D // g.S
    EU = experts * U
    S, X, C, T = g.S, g.X, g.C, g.T
    nm = D // GROUP

    loc = {}

    def local(name, src, dst):
        cp = pltpu.make_async_copy(src, dst, r.lsem.at[len(loc)])
        cp.start()
        loc[name] = cp

    own_rows = pl.ds(pl.multiple_of(w.s * Ds, 16), Ds)
    local("qkv", r.wqkv_h, r.wqkv.at[own_rows])
    local("attn", r.wattn_h, r.wattn.at[own_rows])

    def expin(owner, e, target):
        return (
            r.wexpin_h.at[e, :, pl.ds(pl.multiple_of(target * U, 128), U)],
            r.win.at[pl.ds(pl.multiple_of(owner * Ds, 16), Ds), e * U : (e + 1) * U],
        )

    for e in range(experts):
        src, dst = expin(w.s, e, w.tp)
        local(("in", e), src, dst)
    for e in range(experts):
        local(("out", e), r.wout_h.at[e, pl.ds(pl.multiple_of(w.t * U, 16), U)], r.wout.at[pl.ds(e * U, U)])
    r.SM[w.s] = jnp.zeros((8, Ds), f32)
    r.SM[w.s, 0:experts] = r.gate_t[...].astype(f32)
    r.SM[w.s, experts : experts + 1] = r.n_one[...].astype(f32)
    r.SM[w.s, experts + 1 : experts + 2] = r.n_two[...].astype(f32)
    own = pl.ds(pl.multiple_of(w.tp * n, 16), n)
    r.DO[own] = padded(r.cot, n).astype(bf16)

    greet(w)
    sends = Sends(r.ssem)
    q = Ds // T
    P2 = 2 if q >= 32 else 1

    def piece(ref, s, t, p, base=0):
        return ref.at[pl.ds(pl.multiple_of(base * s * Ds + t * q + p * (q // P2), 16), q // P2)]

    for j in range(1, S):
        sends.go(r.SM.at[w.s], r.SM.at[w.s], r.smsem.at[w.s], w.dev(js=j))
    for p in range(P2):
        for j in range(1, S):
            sends.go(piece(r.wqkv_h, w.s, w.t, p), piece(r.wqkv, w.s, w.t, p, 1), r.qsem.at[w.s, w.t, p], w.dev(js=j))
    half = Ds // C

    def part(ref, s, c, base=0):
        return ref.at[pl.ds(pl.multiple_of(base * s * Ds + c * half, 16), half)]

    for j in range(1, S):
        sends.go(part(r.wattn_h, w.s, w.c), part(r.wattn, w.s, w.c, 1), r.asem.at[w.s, w.c], w.dev(js=j))
    for j in range(1, S):
        for e in range(experts):
            src, dst = expin(w.s, e, w.sj(j) * T + w.t)
            sends.go(src, dst, r.esem.at[w.s, e], w.dev(js=j))

    resid = padded(r.tok, n)
    cen = resid - jnp.mean(resid, axis=-1, keepdims=True)
    r.tmp[...] = cen * lax.rsqrt(jnp.mean(cen * cen, axis=-1, keepdims=True) + NORM_EPS)
    for p in range(P2):
        for j in range(1, S):
            v = piece(r.wqkv, w.sj(j), w.t, p, 1)
            sem = r.qsem.at[w.sj(j), w.t, p]
            arrived(v, sem)
            for jx in range(1, X):
                sends.go(v, v, sem, w.dev(jx=jx))
            for jc in range(1, C):
                sends.go(v, v, sem, w.dev(jc=jc))
    for jx in range(1, X):
        sends.go(r.DO.at[own], r.DO.at[own], r.dsem.at[w.tp], w.dev(jx=jx))
    for jc in range(1, C):
        sends.go(r.DO.at[own], r.DO.at[own], r.dsem.at[w.tp], w.dev(jc=jc))
    for j in range(1, S):
        arrived(r.SM.at[w.sj(j)], r.smsem.at[w.sj(j)])
    for p in range(P2):
        for j in range(1, S):
            for jx in range(1, X):
                t = w.xj(jx) * C + w.c
                v, sem = piece(r.wqkv, w.sj(j), t, p, 1), r.qsem.at[w.sj(j), t, p]
                arrived(v, sem)
                for jc in range(1, C):
                    sends.go(v, v, sem, w.dev(jc=jc))
    loc["qkv"].wait()
    for jc in range(1, C):
        for p in range(P2):
            for j in range(1, S):
                for jx in range(X):
                    t = w.xj(jx) * C + w.cj(jc)
                    arrived(piece(r.wqkv, w.sj(j), t, p, 1), r.qsem.at[w.sj(j), t, p])
    small = jnp.concatenate([r.SM[i] for i in range(S)], axis=-1)
    gain_one = small[experts : experts + 1]
    gain_two = small[experts + 1 : experts + 2]
    h1 = (r.tmp[...] * gain_one).astype(bf16)
    for k in range(3):
        r.proj[0:n, k * D : (k + 1) * D] = nn(h1, r.wqkv[:, k * D : (k + 1) * D]).astype(bf16)
    if g.TK > n:
        r.proj[n : g.TK] = jnp.zeros((g.TK - n, 3 * D), bf16)
    for j in range(1, S):
        v, sem = part(r.wattn, w.sj(j), w.c, 1), r.asem.at[w.sj(j), w.c]
        arrived(v, sem)
        for jc in range(1, C):
            sends.go(v, v, sem, w.dev(jc=jc))
    attention(r.proj, r.attn, r.probs, g)
    loc["attn"].wait()
    for j in range(1, S):
        for jc in range(1, C):
            arrived(part(r.wattn, w.sj(j), w.cj(jc), 1), r.asem.at[w.sj(j), w.cj(jc)])
    r.mixed[...] = padded(r.tok, n) + nn(r.attn[...], r.wattn[...])
    h2, _, _ = layer_norm(r.mixed[...], gain_two)
    r.H[own] = h2.astype(bf16)
    r.WM[w.tp] = jnp.zeros((8, g.TK), f32)
    rt = r.routes[0].astype(f32)
    r.WM[w.tp, :, 0 : g.seq] = gates_of(h2[0 : g.seq], small, rt)

    n0 = n // 32 * 16

    def hv(b, h):
        lo, size = ((0, n0), (n0, n - n0))[h]
        return r.H.at[pl.ds(pl.multiple_of(b * n + lo, 16), size)]

    def h_send(js, jx, h, to):
        b = w.block(js, jx, 0)
        sends.go(hv(b, h), hv(b, h), r.hsem.at[b, h], w.dev(*to))

    def h_wait(js, jx, jc, h):
        b = w.block(js, jx, jc)
        arrived(hv(b, h), r.hsem.at[b, h])

    def h_core(js, jx, h):
        for jc in range(1, C):
            h_send(js, jx, h, (0, 0, jc))

    others = [(a, b, c) for a in range(S) for b in range(X) for c in range(C) if a or b or c]
    for to in others:
        sends.go(r.WM.at[w.tp], r.WM.at[w.tp], r.msem.at[w.tp], w.dev(*to))
    for jx in range(1, X):
        h_send(0, 0, 0, (0, jx))
    for j in range(1, S):
        h_send(0, 0, 1, (j,))
    h_core(0, 0, 0)
    h_core(0, 0, 1)
    for j in range(1, S):
        h_send(0, 0, 0, (j,))
    for jx in range(1, X):
        h_send(0, 0, 1, (0, jx))

    def d_rows(js, jx, jc=0):
        return r.DO.at[pl.ds(pl.multiple_of(w.block(js, jx, jc) * n, 16), n)]

    def d_sem(js, jx, jc=0):
        return r.dsem.at[w.block(js, jx, jc)]

    def d_core(js, jx):
        for jc in range(1, C):
            sends.go(d_rows(js, jx), d_rows(js, jx), d_sem(js, jx), w.dev(jc=jc))

    for jx in range(1, X):
        h_wait(0, jx, 0, 0)
        for j in range(1, S):
            h_send(0, jx, 0, (j,))
        h_core(0, jx, 0)
    for j in range(1, S):
        sends.go(d_rows(0, 0), d_rows(0, 0), d_sem(0, 0), w.dev(js=j))
    for jx in range(1, X):
        arrived(d_rows(0, jx), d_sem(0, jx))
        for j in range(1, S):
            sends.go(d_rows(0, jx), d_rows(0, jx), d_sem(0, jx), w.dev(js=j))
        d_core(0, jx)
    for e in range(experts):
        loc[("in", e)].wait()
        for j in range(1, S):
            _, dst = expin(w.sj(j), e, w.tp)
            arrived(dst, r.esem.at[w.sj(j), e])

    RT = 16

    def map_wait(js, jx, jc):
        b = w.block(js, jx, jc)
        if js or jx or jc:
            arrived(r.WM.at[b], r.msem.at[b])
        return b

    def forward(b, es):
        rows = pl.ds(pl.multiple_of(b * n, 16), n)
        r.COL[...] = turned(r.WM[b])
        for e in es:
            cols = slice(e * U, (e + 1) * U)
            r.INN[:, cols] = nn(r.H[rows], r.win[:, cols])
            for i in range(n // RT):
                o = pl.ds(pl.multiple_of(b * n + i * RT, RT), RT)
                v = r.INN[i * RT : (i + 1) * RT, cols]
                cdf, pdf = erf_parts(v)
                gate = r.COL[i * RT : (i + 1) * RT, e : e + 1]
                r.ACT[o, cols] = (v * cdf * gate).astype(bf16)
                r.DG[o, cols] = ((cdf + v * pdf) * gate).astype(bf16)

    every = list(range(experts))
    forward(w.block(0, 0, 0), every)
    for jc in range(1, C):
        h_wait(0, 0, jc, 0)
        h_wait(0, 0, jc, 1)
        forward(map_wait(0, 0, jc), every)
    for jx in range(1, X):
        h_wait(0, jx, 0, 1)
        h_core(0, jx, 1)
    for j in range(1, S):
        h_wait(j, 0, 0, 1)
        for jx in range(1, X):
            h_send(j, 0, 1, (0, jx))
        h_core(j, 0, 1)
    for jx in range(1, X):
        forward(map_wait(0, jx, 0), every)
        for jc in range(1, C):
            h_wait(0, jx, jc, 0)
            h_wait(0, jx, jc, 1)
            forward(map_wait(0, jx, jc), every)
    late = [(a, b, c) for a in range(1, S) for b in range(X) for c in range(C)]
    for j in range(1, S):
        for jx in range(X):
            h_wait(j, jx, 0, 0)
            h_core(j, jx, 0)
        for jx in range(1, X):
            h_wait(j, jx, 0, 1)
            h_core(j, jx, 1)
    for j in range(1, S):
        for jc in range(1, C):
            for jx in range(X):
                h_wait(j, jx, jc, 0)
                h_wait(j, jx, jc, 1)
    for at in late:
        map_wait(*at)
    tail = Tail(g, w, experts, D, r)
    per = g.NO // experts

    for e in range(experts):
        for at in late:
            forward(w.block(*at), [e])
        if e == 0:
            for j in range(1, S):
                for jx in range(X):
                    arrived(d_rows(j, jx), d_sem(j, jx))
                    d_core(j, jx)
            for jc in range(1, C):
                for j in range(S):
                    for jx in range(X):
                        arrived(d_rows(j, jx, jc), d_sem(j, jx, jc))
        v = tn(r.ACT[:, e * U : (e + 1) * U], r.DO[...])
        k = 0
        for u in range(U // g.CR):
            for c in range(D // 256):
                r.G[e * per + k] = v[u * g.CR : (u + 1) * g.CR, c * 256 : (c + 1) * 256]
                k += 1
        tail.ready = (e + 1) * per
        tail.serve(2)

    for e in range(experts):
        loc[("out", e)].wait()
    ph = Scatter(w, sends, r.PH, n, r.rs_h, r.ph_s)
    po = Scatter(w, sends, r.PO, n, r.rs_o, r.po_s)
    pick = (
        lax.broadcasted_iota(jnp.int32, (8, experts * 128), 0)
        == lax.broadcasted_iota(jnp.int32, (8, experts * 128), 1) // 128
    ).astype(f32).astype(bf16)

    def backward(b):
        rows = pl.ds(pl.multiple_of(b * n, 16), n)
        for e in every:
            cols = slice(e * U, (e + 1) * U)
            r.INN[:, cols] = nt(r.DO[rows], r.wout[cols])
            for i in range(n // RT):
                o = pl.ds(pl.multiple_of(b * n + i * RT, RT), RT)
                m = slice(i * RT, (i + 1) * RT)
                v = r.INN[m, cols]
                a = r.ACT[o, cols].astype(f32) * v
                r.DIN[o, cols] = (r.DG[o, cols].astype(f32) * v).astype(bf16)
                t = a[:, 0:128]
                for z in range(1, U // 128):
                    t = t + a[:, z * 128 : (z + 1) * 128]
                r.GS[m, e * 128 : (e + 1) * 128] = t
        ga, gb, _ = split3(r.GS[...])
        r.DW[b] = jnp.zeros((8, g.TK), f32)
        r.DW[b, :, 0:n] = nt(pick, ga) + nt(pick, gb)
        r.PH[rows] = nt(r.DIN[rows], r.win[...]).astype(bf16)

    far = [(a, b) for a in reversed(range(S)) for b in reversed(range(X))]
    for jc in range(1, C):
        for js, jx in far:
            backward(w.block(js, jx, jc))
            ph.core_send(js, jx)
            tail.serve(1)
    for js, jx in far:
        backward(w.block(js, jx, 0))
        ph.core_add(js, jx)
        if js:
            ph.s_send(js, jx)
        tail.serve(1)
    for to in others:
        sends.go(r.DW.at[w.block(*to)], r.DWr.at[w.tp], r.wsem.at[w.tp], w.dev(*to))
    for e in range(experts):
        v = tn(r.H[...], r.DIN[:, e * U : (e + 1) * U])
        for s in range(S):
            j = lax.rem(s - w.s + S, S)
            for u in range(Ds // g.CR):
                lo = s * Ds + u * g.CR
                r.G[g.NO + (e * (Ds // g.CR) + u) * S + j] = v[lo : lo + g.CR]
        tail.ready = g.NO + (e + 1) * (Ds // g.CR) * S
        tail.serve(1)
    for jx in range(1, X):
        ph.x_send(jx)

    def out_block(js, jx, jc):
        rows = po.rows(js, jx, jc)
        r.PO[rows] = nn(r.ACT[rows], r.wout[...]).astype(bf16)

    for jc in range(1, C):
        for js, jx in far:
            out_block(js, jx, jc)
            po.core_send(js, jx)
            tail.serve(1)

    dh2 = ph.result()
    gdg = r.DW[w.tp]
    for at in others:
        b = w.block(*at)
        arrived(r.DWr.at[b], r.wsem.at[b])
        gdg = gdg + r.DWr[b]
    dlt = (gdg - r.WM[w.tp] * jnp.sum(gdg, axis=0, keepdims=True))[:, 0:n]
    small_low = small.astype(bf16)
    da, db, dc = split3(dlt)
    dh2 = dh2 + tn(da, small_low) + tn(db, small_low) + tn(dc, small_low)
    h2, xhat2, r2 = layer_norm(r.mixed[...], gain_two)
    ha, hb, _ = split3(h2)
    ggate = nn(da, ha) + nn(db, ha) + nn(da, hb)
    gtwo = jnp.sum(dh2 * xhat2, axis=0, keepdims=True)
    dmixed = padded(r.cot, n) + norm_back(dh2, xhat2, r2, gain_two)
    r.tmp[...] = dmixed
    dlow = dmixed.astype(bf16)
    r.dattn[...] = nt(dlow, r.wattn[...]).astype(bf16)
    r.M[:, 3 * D : 4 * D] = tn(r.attn[...], dlow).astype(bf16)
    tail.serve(1)
    attention_back(r.proj, r.probs, r.dattn, r.dproj, g, tail.serve)
    h1, xhat1, r1 = layer_norm(padded(r.tok, n), gain_one)
    h1b = h1.astype(bf16)
    for k in range(3):
        r.M[:, k * D : (k + 1) * D] = tn(h1b, r.dproj[:, k * D : (k + 1) * D]).astype(bf16)
    ms = Scatter(w, sends, r.M, nm, r.rs_m, r.m_s)
    for jc in range(1, C):
        for js, jx in far:
            ms.core_send(js, jx)
    tail.serve(1)
    dh1 = nt(r.dproj[...], r.wqkv[...])
    gone = jnp.sum(dh1 * xhat1, axis=0, keepdims=True)
    r.gtok[0] = (r.tmp[...] + norm_back(dh1, xhat1, r1, gain_one))[0 : g.seq].astype(bf16)
    for s in range(S):
        cols = slice(s * Ds, (s + 1) * Ds)
        r.SG[s, 0:8] = ggate[:, cols]
        r.SG[s, experts : experts + 1] = gone[:, cols]
        r.SG[s, experts + 1 : experts + 2] = gtwo[:, cols]
    for to in others:
        sends.go(r.SG.at[w.sj(to[0])], r.SGr.at[w.tp], r.sgsem.at[w.tp], w.dev(*to))
    for js, jx in far:
        ms.core_add(js, jx)
        if js:
            ms.s_send(js, jx)
    tail.serve(1)
    for js, jx in far:
        out_block(js, jx, 0)
        po.core_add(js, jx)
        if js:
            po.s_send(js, jx)
        tail.serve(1)
    for jx in range(1, X):
        ms.x_send(jx)
    tail.serve(1)
    for jx in range(1, X):
        po.x_send(jx)
    tail.serve(1)
    m = ms.result()
    base = g.NO + g.NI
    wide = g.CR // nm
    for k in range(g.NM):
        for i in range(wide):
            c = (k * wide + i) * 256
            r.G[base + k, i * nm : (i + 1) * nm] = m[:, c : c + 256]
    sg = r.SG[w.s]
    for at in others:
        b = w.block(*at)
        arrived(r.SGr.at[b], r.sgsem.at[b])
        sg = sg + r.SGr[b]
    r.G[g.NO + g.NI + g.NM] = jnp.zeros((g.CR, 256), f32)
    r.G[g.NO + g.NI + g.NM, 0:8, 0:Ds] = sg
    tail.ready = tail.n
    tail.serve(1)
    r.out[0] = (r.mixed[...] + po.result())[0 : g.seq].astype(bf16)

    @pl.loop(tail.i, tail.total)
    def _(i):
        tail.step(i)

    tail.finish()
    sends.finish()


def on_device(mesh, tokens, norm_one, w_qkv, w_attn, norm_two, w_gate, w_expin, w_expout, routes, cotangent):
    g = geometry(mesh, tokens.shape, w_expout.shape[1] * mesh.shape["shard"])
    experts = w_expin.shape[0]
    D = tokens.shape[2]
    Ds, U, n = D // g.S, g.U, g.TP
    N = GROUP * n
    EU = experts * U
    nm = D // GROUP
    g.LAG = 2
    g.NO = experts * (U // g.CR) * (D // 256)
    g.NI = g.S * experts * (Ds // g.CR)
    g.NM = nm * 4 * D // (g.CR * 256)
    NC = g.NO + g.NI + g.NM + 1
    dma = pltpu.SemaphoreType.DMA
    vm = pl.BlockSpec(memory_space=pltpu.VMEM)
    hb = pl.BlockSpec(memory_space=pl.ANY)
    sds = jax.ShapeDtypeStruct
    V = pltpu.VMEM
    ins = dict(
        tok=(tokens, vm), cot=(cotangent, vm), routes=(jnp.swapaxes(routes, 1, 2), vm), gate_t=(w_gate.T, vm),
        n_one=(norm_one.reshape(1, Ds), vm), n_two=(norm_two.reshape(1, Ds), vm), wqkv_h=(w_qkv, hb),
        wattn_h=(w_attn, hb), wexpin_h=(w_expin, hb), wout_h=(w_expout, hb),
    )
    outs = dict(
        out=sds(tokens.shape, bf16), gtok=sds(tokens.shape, bf16), FO=sds((experts, U * g.T, D), bf16),
        FI=sds((experts, Ds, U * GROUP), bf16), FM=sds((g.T, g.NM, g.CR, 256), bf16), SGo=sds((8, Ds), f32),
    )
    rs_h, ph_s = Scatter.scratch(g, n, D)
    rs_o, po_s = Scatter.scratch(g, n, D)
    rs_m, m_s = Scatter.scratch(g, nm, 4 * D)
    S, T = g.S, g.T
    scr = dict(
        H=V((N, D), bf16), DO=V((N, D), bf16), WM=V((GROUP, 8, g.TK), f32), win=V((D, EU), bf16), wout=V((EU, D), bf16),
        wqkv=V((D, 3 * D), bf16), wattn=V((D, D), bf16), SM=V((S, 8, Ds), f32), proj=V((g.TK, 3 * D), bf16),
        attn=V((n, D), bf16), probs=V((HEADS, n, g.TK), f32), mixed=V((n, D), f32), tmp=V((n, D), f32),
        COL=V((g.TK, 128), f32), INN=V((n, EU), f32), ACT=V((N, EU), bf16), DG=V((N, EU), bf16), DIN=V((N, EU), bf16),
        GS=V((n, experts * 128), f32), PO=V((N, D), bf16), PH=V((N, D), bf16), DW=V((GROUP, 8, g.TK), f32),
        DWr=V((GROUP, 8, g.TK), f32), dattn=V((n, D), bf16), dproj=V((n, 3 * D), bf16), M=V((D, 4 * D), bf16),
        SG=V((S, 8, Ds), f32), SGr=V((GROUP, 8, Ds), f32), G=V((NC, g.CR, 256), f32), RU=V((NC, g.CR, 256), bf16),
        RD=V((NC, g.CR, 256), bf16), SU=V((NC, g.CR, 256), bf16), SD=V((NC, g.CR, 256), bf16), tot=V((g.CR, 256), f32),
        rs_h=rs_h, rs_o=rs_o, rs_m=rs_m, ph_s=ph_s, po_s=po_s, m_s=m_s,
        ssem=dma((160,)), lsem=dma((2 + 2 * experts,)), smsem=dma((S,)), qsem=dma((S, T, 2)), asem=dma((S, g.C)),
        esem=dma((S, experts)), dsem=dma((GROUP,)), hsem=dma((GROUP, 2)), msem=dma((GROUP,)), wsem=dma((GROUP,)),
        sgsem=dma((GROUP,)), chain_s=[dma((NC,))] * 4, fsend=dma((5, NC)), fo=dma((T, g.NO)), fi=dma((GROUP, g.NI // S)),
        fm=dma((T, g.NM)),
    )
    leaves, tree = jax.tree.flatten(scr, is_leaf=lambda v: not isinstance(v, (list, dict)))

    def body(*refs):
        a, b = len(ins), len(ins) + len(outs)
        r = SimpleNamespace(**dict(zip(ins, refs[:a])), **dict(zip(outs, refs[a:b])), **jax.tree.unflatten(tree, refs[b:]))
        whole_step(g, experts, r)

    res = pl.pallas_call(
        body,
        name="step",
        out_shape=list(outs.values()),
        in_specs=[v[1] for v in ins.values()],
        out_specs=[vm] * len(outs),
        scratch_shapes=leaves,
        compiler_params=pltpu.CompilerParams(collective_id=0, has_side_effects=True, vmem_limit_bytes=VMEM_BYTES),
    )(*[v[0] for v in ins.values()])
    out, gtok, FO, FI, FM, SGo = res
    wide = g.CR // nm
    fm = FM.reshape(g.T, g.NM * wide, nm, 256).swapaxes(1, 2).reshape(Ds, 4 * D)
    return (
        out, gtok, SGo[experts], fm[:, : 3 * D].astype(f32), fm[:, 3 * D :].astype(f32), SGo[experts + 1],
        SGo[:experts].T, FI.astype(f32), FO.astype(f32),
    )


def solution(mesh):
    placed = (
        P(("rep", "shard"), None, None), P("shard"), P("shard", None), P("shard", None), P("shard"), P("shard", None),
        P(None, "shard", None), P(None, "shard", None), P(("rep", "shard"), None, None), P(("rep", "shard"), None, None),
    )
    return jax.shard_map(
        partial(on_device, mesh),
        mesh=mesh,
        in_specs=placed,
        out_specs=(
            P(("rep", "shard"), None, None), P(("rep", "shard"), None, None), P("shard"), P("shard", None),
            P("shard", None), P("shard"), P("shard", None), P(None, "shard", None), P(None, "shard", None),
        ),
        check_vma=False,
    )
```
